32 devices in a mesh: parts: 2 (over y), seq: 4 (over z), chan: 4 (over x, core).
Axes of the slice: x: 2, y: 2, z: 4, core: 2. Of those that a mesh axis runs over, the one named last changes fastest.
Arguments:
- records: bfloat16 [8, 1536, 512], P('parts', 'seq', 'chan'), parts along dimension 0, may hold values from -6 to 6
- norm_gain: float32 [512], replicated, may hold values from 0.1 to 1.9
- in_projection: bfloat16 [512, 3, 512], P(None, None, 'chan'), may hold values from -0.25 to 0.25
- short_kernel: float32 [3, 3, 512], P(None, None, 'chan'), may hold values from -3.5 to 3.5
- long_filter: bfloat16 [16, 1536], P('chan', 'seq'), may hold values from -1.6 to 1.6
- skip_gain: float32 [512], P('chan'), may hold values from 0.5 to 1.5
- out_projection: bfloat16 [512, 512], P('chan'), may hold values from -0.25 to 0.25
Outputs:
- mixed: bfloat16 [8, 1536, 512], P('parts', 'seq', 'chan'), parts along dimension 0
The draws below stay inside these ranges and needn't reach their ends.
There are 2 independent parts, one for each index of `parts`. The reference program is written for one: setup_inputs(seed, part) draws one part's arguments, and reference() takes and returns one part's arrays. A program takes and returns all parts, laid end to end along the dimension named above; an argument that names none is the same for every part. Nothing has to cross between parts.
All inputs are finite; a program needn't handle non-finite values.
Results may differ from the reference program's by a relative error of at most 0.015.
Values may be sent and summed in bfloat16 or wider, within the bound.
A program may use at most 128 MiB of HBM per device.

```python
import jax
import jax.numpy as jnp
from jax import lax

D = 512
FGROUP = 32
RECS = 4
FILTERS = 16
LENGTH = 1536


def draw_long_filter(key, part):
    first_key, second_key, level_key, sign_key = jax.random.split(jax.random.fold_in(key, 11), 4)
    picked = jax.random.uniform(first_key, (FILTERS, 1), dtype=jnp.float32)
    reach = jnp.exp(jnp.log(20.0) + picked * (jnp.log(4.0 * LENGTH) - jnp.log(20.0)))
    noise = jnp.clip(jax.random.normal(second_key, (FILTERS, LENGTH), dtype=jnp.float32), -5.0, 5.0)
    lags = jnp.arange(LENGTH, dtype=jnp.float32)[None, :]
    amplitude = 1.0 / jnp.sqrt(jnp.minimum(0.5 * reach + 1.0, LENGTH * 1.0))
    magnitude = jax.random.uniform(level_key, (FILTERS, 1), dtype=jnp.float32, minval=1.5, maxval=3.0)
    signs = jax.random.bernoulli(sign_key, 0.5, (FILTERS, 1)).astype(jnp.float32) * 2.0 - 1.0
    tail_part = magnitude * signs / LENGTH * jnp.exp(-lags / (3.0 * LENGTH))
    return (noise * jnp.exp(-lags / reach) * amplitude + tail_part).astype(jnp.bfloat16)


def draw_records(key, part):
    common_key, noise_key = jax.random.split(jax.random.fold_in(key, 23), 2)
    common = jax.random.normal(common_key, (RECS, 1, D), dtype=jnp.float32)
    noise = jnp.clip(jax.random.normal(noise_key, (RECS, LENGTH, D), dtype=jnp.float32), -5.0, 5.0)
    values = 0.8 * common + 0.8 * noise
    return jnp.clip(values, -6.0, 6.0).astype(jnp.bfloat16)


def levels(stream_key, shape, pieces, smallest, largest):
    def one(dim, shards_of):
        steps = jax.random.uniform(jax.random.fold_in(jax.random.fold_in(stream_key, 6), dim), (shards_of,), jnp.float32, smallest / len(pieces), largest / len(pieces))
        return jnp.repeat(jnp.exp(steps), shape[dim] // shards_of).reshape((-1,) + (1,) * (len(shape) - dim - 1))

    level = one(*pieces[0])
    for cut in pieces[1:]:
        level = level * one(*cut)
    return level


def bell_draw(stream_key, shape, width, most, cuts=(), kind=jnp.bfloat16):
    entries = jax.random.normal(stream_key, shape, jnp.float32) * width
    if len(cuts) > 0:
        entries = levels(stream_key, shape, cuts, -0.22, 0.18) * entries
    return jnp.clip(entries, min=-most, max=most).astype(kind)


def setup_inputs(seed: int = 0, part: int = 0) -> dict:
    key_list = jax.random.split(jax.random.key(seed), 8)
    part_keys = jax.random.split(jax.random.fold_in(key_list[7], part), 8)
    return {
        "records": draw_records(jax.random.fold_in(jax.random.fold_in(key_list[7], part), 71), part),
        "norm_gain": jnp.clip(1.0 + 0.18 * jax.random.normal(key_list[1], (D,), jnp.float32), 0.1, 1.9),
        "in_projection": bell_draw(key_list[2], (D, 3, D), D ** -0.5, 0.25, ((2, 4),)),
        "short_kernel": bell_draw(key_list[3], (3, 3, D), 3 ** -0.5, 3.5, ((2, 4),), jnp.float32),
        "long_filter": draw_long_filter(jax.random.fold_in(key_list[7], 71), part),
        "skip_gain": jnp.clip(0.5 + 1.0 * jax.random.uniform(key_list[5], (D,), jnp.float32) ** levels(key_list[5], (D,), ((0, 4),), -0.2, 0.2), 0.5, 1.5),
        "out_projection": bell_draw(key_list[6], (D, D), D ** -0.5, 0.25, ((0, 4),)),
    }


def reference(records, norm_gain, in_projection, short_kernel, long_filter, skip_gain, out_projection):
    widened = records.astype(jnp.float32)
    inv_rms = lax.rsqrt(lax.optimization_barrier(jnp.mean(widened * widened, axis=-1, keepdims=True)) + 1e-06)
    normed = (widened * inv_rms * norm_gain).astype(jnp.bfloat16)
    projected = jnp.einsum('rtd,dkc->rtkc', normed.astype(jnp.float32), in_projection.astype(jnp.float32)).astype(jnp.bfloat16)
    extended = jnp.pad(projected.astype(jnp.float32), ((0, 0), (2, 0), (0, 0), (0, 0)))
    streams = short_kernel[0] * extended[:, 2:] + short_kernel[1] * extended[:, 1:-1] + short_kernel[2] * extended[:, :-2]
    query_gate = streams[:, :, 0]
    gated_source = (streams[:, :, 1] * streams[:, :, 2]).astype(jnp.bfloat16)
    per_channel = jnp.repeat(long_filter.astype(jnp.float32), FGROUP, axis=0).T
    filter_spec = jnp.fft.rfft(per_channel, n=2 * LENGTH, axis=0)

    def convolve(signal):
        spectrum = jnp.fft.rfft(signal, n=2 * LENGTH, axis=0) * filter_spec
        return jnp.fft.irfft(spectrum, n=2 * LENGTH, axis=0)[:LENGTH]
    widened_source = gated_source.astype(jnp.float32)
    long_out = lax.map(convolve, widened_source) + skip_gain * widened_source
    gated = (query_gate * long_out).astype(jnp.bfloat16)
    mixed = jnp.einsum('rtc,cd->rtd', gated.astype(jnp.float32), out_projection.astype(jnp.float32))
    return mixed.astype(jnp.bfloat16)
```

```python
import functools

import jax
import jax.numpy as jnp
from jax import lax
from jax.experimental import pallas as pl
from jax.experimental.pallas import tpu as pltpu
from jax.sharding import PartitionSpec as P


def from_behind(block, axis, distance):
    devices = range(lax.axis_size(axis))
    route = [(i - distance, i) for i in devices if i - distance in devices]
    return lax.ppermute(block, axis, route)


def block_terms(taps_padded, offset, block_source, block_len):
    filter_count = taps_padded.shape[0]
    window = lax.dynamic_slice_in_dim(taps_padded, offset + 1, 2 * block_len - 1, 1)
    flipped = window[:, ::-1]
    padded = jnp.pad(flipped, ((0, 0), (0, 1)))
    tiled_taps = jnp.tile(padded, (1, block_len))
    toeplitz = tiled_taps[:, block_len - 1 : block_len - 1 + block_len * (2 * block_len - 1)]
    toeplitz = toeplitz.reshape(filter_count, block_len, 2 * block_len - 1)[:, :, :block_len]
    record_count = block_source.shape[0]
    grouped = block_source.reshape(record_count, block_len, filter_count, -1)
    return jnp.einsum("fab,rbfg->rafg", toeplitz, grouped, preferred_element_type=jnp.float32)


def body(records, norm_gain, in_projection, short_kernel, long_filter, skip_gain, out_projection):
    gathered = lax.all_gather(records, "chan", axis=2, tiled=True)
    widened = gathered.astype(jnp.float32)
    inv_rms = lax.rsqrt(jnp.mean(widened * widened, axis=-1, keepdims=True) + 1e-06)
    normed = (widened * inv_rms * norm_gain).astype(jnp.bfloat16)
    projected = jnp.einsum(
        "rtd,dkc->rtkc", normed, in_projection, preferred_element_type=jnp.float32
    ).astype(jnp.bfloat16)
    rim_rows = from_behind(projected[:, -2:], "seq", 1)
    extended = jnp.concatenate([rim_rows, projected], axis=1).astype(jnp.float32)
    streams = (
        short_kernel[0] * extended[:, 2:]
        + short_kernel[1] * extended[:, 1:-1]
        + short_kernel[2] * extended[:, :-2]
    )
    query_gate = streams[:, :, 0]
    gated_source = (streams[:, :, 1] * streams[:, :, 2]).astype(jnp.bfloat16)
    record_count = gated_source.shape[0]
    block_len = gated_source.shape[1]
    channels = gated_source.shape[2]
    all_taps = lax.all_gather(long_filter, "seq", axis=1, tiled=True)
    taps_padded = jnp.concatenate(
        [jnp.zeros((all_taps.shape[0], block_len), jnp.bfloat16), all_taps], axis=1
    )
    my_start = lax.axis_index("seq") * block_len
    cycle_stops = lax.axis_size("seq")
    long_sum = block_terms(taps_padded, 0, gated_source, block_len)

    def advance(stop_index, state):
        running_sum, visiting = state
        visiting = from_behind(visiting, "seq", 1)
        lag_start = stop_index * block_len
        running_sum = lax.cond(
            lag_start <= my_start,
            lambda running: running + block_terms(taps_padded, lag_start, visiting, block_len),
            lambda running: running,
            running_sum,
        )
        return (running_sum, visiting)

    long_sum, visiting = lax.fori_loop(1, cycle_stops, advance, (long_sum, gated_source))
    long_out = long_sum.reshape(
        record_count, block_len, channels
    ) + skip_gain * gated_source.astype(jnp.float32)
    gated = (query_gate * long_out).astype(jnp.bfloat16)
    partial_terms = jnp.einsum(
        "rtc,cd->rtd", gated, out_projection, preferred_element_type=jnp.float32
    )
    return lax.psum_scatter(
        partial_terms.astype(jnp.bfloat16), "chan", scatter_dimension=2, tiled=True
    )


MESH = pl.DeviceIdType.MESH


def layer_kernel(
    n_seq, n_chan, recs_ref, gain_hbm, w_in_hbm, short_hbm, taps_ref, skip_hbm, w_out_ref, out_ref,
    gain_ref, w_in_ref, short_ref, skip_ref, first, stage, peer, proj, taps, strips, source, gated, second,
    w_out, mixed,
    z_send, z_recv, x_send, x_recv, m_send, p_send, p_recv, g_send, g_recv, o_send, o_recv,
    f_send, f_recv, w_send, w_recv, here_sem,
):
    block_len, width = recs_ref.shape[1], recs_ref.shape[2]
    length = n_seq * block_len
    filters = taps_ref.shape[0]
    group = width // filters
    half = width // 2
    per_block = block_len // width
    chunks = n_seq * per_block
    z = lax.axis_index("seq")
    c = lax.axis_index("chan")
    core = c % 2
    here = c - core
    there = (here + n_chan // 2) % n_chan
    core_mate = here + 1 - core
    chip_mate = there + core

    barrier = pltpu.get_barrier_semaphore()
    for d in range(1, n_seq):
        for k in range(2):
            pl.semaphore_signal(
                barrier, inc=1, device_id={"seq": (z + d) % n_seq, "chan": here + k}, device_id_type=MESH
            )
    for d in range(1, n_chan):
        pl.semaphore_signal(barrier, inc=1, device_id={"chan": (c + d) % n_chan}, device_id_type=MESH)
    pl.semaphore_wait(barrier, 2 * (n_seq - 1) + n_chan - 1)

    def remote(src, dst, send, recv, **device):
        return pltpu.make_async_remote_copy(
            src_ref=src, dst_ref=dst, send_sem=send, recv_sem=recv, device_id=device, device_id_type=MESH
        )

    def rows(part, k):
        return pl.ds(pl.multiple_of(part * width + k * half, half), half)

    def f_copy(d):
        return remote(taps_ref, taps.at[z], f_send.at[d], f_recv.at[d], seq=(z + d) % n_seq)

    def z_copy(r, part, k):
        return remote(
            recs_ref.at[r, rows(part, k)], first.at[z * per_block + part, c],
            z_send.at[r, part, k], z_recv.at[z * per_block + part], seq=r, chan=here + k,
        )

    def own_local(part):
        i = z * per_block + part
        return pltpu.make_async_copy(recs_ref.at[z, rows(part, core)], first.at[i, c], z_recv.at[i])

    def own_mate(part):
        i = z * per_block + part
        return remote(
            recs_ref.at[z, rows(part, 1 - core)], first.at[i, c], m_send.at[part], z_recv.at[i], chan=core_mate
        )

    def own_x(part, k):
        i = z * per_block + part
        return remote(
            recs_ref.at[z, rows(part, k)], first.at[i, c], x_send.at[i, k], x_recv.at[i], chan=there + k
        )

    def x_copy(i):
        held = first.at[i, pl.ds(here, 2)]
        return remote(held, held, x_send.at[i, 0], x_recv.at[i], chan=chip_mate)

    def z_wait(i):
        held = first.at[i, pl.ds(here, 2)]
        remote(held, held, x_send.at[i, 0], z_recv.at[i], chan=chip_mate).wait_recv()

    def x_wait(i):
        held = first.at[i, pl.ds(there, 2)]
        remote(held, held, x_send.at[i, 0], x_recv.at[i], chan=chip_mate).wait_recv()

    def p_copy(i):
        return remote(stage.at[i], peer.at[i], p_send.at[i], p_recv.at[i], chan=core_mate)

    def g_copy(i, k):
        return remote(gated.at[i, k], second.at[i, c], g_send.at[i, k], g_recv.at[i], chan=there + k)

    def g_mate(i):
        return remote(gated.at[i, 1 - core], second.at[i, c], g_send.at[i, 2], g_recv.at[i], chan=core_mate)

    def g_wait(i):
        held = second.at[i, pl.ds(0, 3)]
        remote(held, held, g_send.at[i, 0], g_recv.at[i], chan=core_mate).wait_recv()

    def o_copy(i, j, b):
        part = i - b * per_block
        return remote(
            mixed.at[i, j], out_ref.at[z, rows(part, core)], o_send.at[i, j], o_recv.at[z],
            seq=b, chan=core_mate if j else c,
        )

    def o_mate(i, b):
        part = i - b * per_block
        return remote(
            mixed.at[i, 1], out_ref.at[z, rows(part, core)], o_send.at[i, 1], o_recv.at[z], chan=core_mate
        )

    def o_local(i, b):
        part = i - b * per_block
        return pltpu.make_async_copy(mixed.at[i, 0], out_ref.at[z, rows(part, core)], o_recv.at[z])

    def columns(q):
        return pl.ds(pl.multiple_of(q * width, width), width)

    def w_x(j):
        owner = chip_mate if j == 0 else there + 1 - core
        return remote(
            w_out_ref.at[:, columns(owner)], w_out.at[j, columns(c)], w_send.at[j], w_recv.at[j], chan=chip_mate
        )

    def w_mate(j):
        owner = core_mate if j == 0 else c
        return remote(
            w_out_ref.at[:, columns(owner)], w_out.at[j, columns(c)],
            w_send.at[2 + j], w_recv.at[2 + j], chan=core_mate,
        )

    def w_relay(j):
        return remote(
            w_out.at[1 - j, columns(chip_mate)], w_out.at[j, columns(chip_mate)],
            w_send.at[4 + j], w_recv.at[4 + j], chan=core_mate,
        )

    def w_local(j):
        owner = c if j == 0 else core_mate
        return pltpu.make_async_copy(w_out_ref.at[:, columns(owner)], w_out.at[j, columns(c)], here_sem.at[j])

    own_taps = pltpu.make_async_copy(taps_ref, taps.at[z], here_sem.at[2])
    own_w_in = pltpu.make_async_copy(w_in_hbm, w_in_ref.at[0], here_sem.at[3])
    mate_w_in = remote(w_in_hbm, w_in_ref.at[1], w_send.at[6], w_recv.at[6], chan=core_mate)
    fetched = [
        pltpu.make_async_copy(src, dst, here_sem.at[4 + j])
        for j, (src, dst) in enumerate([(gain_hbm, gain_ref), (short_hbm, short_ref), (skip_hbm, skip_ref)])
    ]

    for d in range(1, n_seq):
        f_copy(d).start()
    for part in range(per_block):
        for k in range(2):
            own_x(part, k).start()
        for r in range(n_seq):

            @pl.when(r != z)
            def _():
                for k in range(2):
                    z_copy(r, part, k).start()

    for part in range(per_block):
        own_local(part).start()
        own_mate(part).start()
    own_taps.start()
    own_w_in.start()
    mate_w_in.start()
    for copy in fetched:
        copy.start()
    for j in range(2):
        w_x(j).start()
        w_mate(j).start()
        w_local(j).start()

    def build_strips():
        own_taps.wait()
        for d in range(1, n_seq):
            f_copy(d).wait_recv()
        rows = lax.broadcasted_iota(jnp.int32, (width, width), 0)
        columns = lax.broadcasted_iota(jnp.int32, (width, width), 1)
        mirror = jnp.where(rows + columns == width - 1, 1.0, 0.0).astype(jnp.bfloat16)
        pieces = []
        for s in reversed(range(n_seq)):
            held = taps[s]
            for j in reversed(range(block_len // width)):
                pieces.append(
                    jnp.dot(held[:, j * width : (j + 1) * width], mirror, preferred_element_type=jnp.float32)
                )
        pieces.append(jnp.zeros((filters, width), jnp.float32))
        backward = jnp.concatenate(pieces, axis=1)
        for f in range(filters):
            row = jnp.broadcast_to(backward[f : f + 1], (width, length + width))
            turned = pltpu.roll(row, 1, 1, stride=1, stride_axis=0)
            strips[f * width : (f + 1) * width, :] = turned[:, width:].astype(jnp.bfloat16)

    def proj_rows(i, k):
        return pl.ds(pl.multiple_of(8 + i * width + k * half, 8), half)

    def spread(i):
        @pl.when(i // per_block != z)
        def _():
            z_wait(i)
            x_copy(i).start()

    def project(i):
        @pl.when(i // per_block == z)
        def _():
            z_wait(i)

        x_wait(i)
        wide = jnp.concatenate([first[i, q] for q in range(n_chan)], axis=1).astype(jnp.float32)
        inv_rms = lax.rsqrt(jnp.mean(wide * wide, axis=-1, keepdims=True) + 1e-06)
        normed = (wide * inv_rms * gain_ref[...]).astype(jnp.bfloat16)
        weights = jnp.concatenate([w_in_ref[j, k] for j in range(2) for k in range(3)], axis=1)
        got = jnp.dot(normed, weights, preferred_element_type=jnp.float32).astype(jnp.bfloat16)
        stage[i] = got[:, 3 * width :]
        p_copy(i).start()
        proj[proj_rows(i, core), :] = got[:, : 3 * width].astype(jnp.float32)

    def convolve(i):
        p_copy(i).wait_recv()
        proj[proj_rows(i, 1 - core), :] = peer[i].astype(jnp.float32)
        short = [jnp.concatenate([short_ref[j, k : k + 1] for k in range(3)], axis=1) for j in range(3)]
        lane_group = lax.broadcasted_iota(jnp.int32, (width, width), 1) // group
        now = proj[8 + i * width : 8 + (i + 1) * width, :]
        back1 = proj[7 + i * width : 7 + (i + 1) * width, :]
        back2 = proj[6 + i * width : 6 + (i + 1) * width, :]
        streams = short[0] * now + short[1] * back1 + short[2] * back2
        query = streams[:, 0:width]
        src = (streams[:, width : 2 * width] * streams[:, 2 * width :]).astype(jnp.bfloat16)
        source[i * width : (i + 1) * width, :] = src
        depth = (i + 1) * width
        sums = jnp.dot(strips[:, length - depth :], source[0:depth, :], preferred_element_type=jnp.float32)
        total = sums[0:width]
        for f in range(1, filters):
            total = jnp.where(lane_group == f, sums[f * width : (f + 1) * width], total)
        total = total + skip_ref[...] * src.astype(jnp.float32)
        result = (query * total).astype(jnp.bfloat16)
        for k in range(2):
            gated[i, k] = result[k * half : (k + 1) * half]
        for k in range(2):
            g_copy(i, k).start()
        g_mate(i).start()
        second[i, c] = gated[i, core]

    def mix(i):
        b = i // per_block
        g_wait(i)
        wide = jnp.concatenate([second[i, q] for q in range(n_chan)], axis=1)
        weights = jnp.concatenate([w_out[0], w_out[1]], axis=1)
        got = jnp.dot(wide, weights, preferred_element_type=jnp.float32).astype(jnp.bfloat16)
        for j in range(2):
            mixed[i, j] = got[:, j * width : (j + 1) * width]

        @pl.when(b == z)
        def _():
            o_local(i, b).start()
            o_mate(i, b).start()

        @pl.when(b != z)
        def _():
            for j in range(2):
                o_copy(i, j, b).start()

    proj[0:8, :] = jnp.zeros((8, proj.shape[1]), jnp.float32)
    for step in range(chunks + 5):
        if step < chunks:
            spread(step)
        if step == 1:
            build_strips()
        if step == 2:
            own_w_in.wait()
            mate_w_in.wait_recv()
            for copy in fetched:
                copy.wait()
        if step == 4:
            for j in range(2):
                w_x(j).wait_recv()
            for j in range(2):
                w_relay(j).start()
        if step == 5:
            for j in range(2):
                w_local(j).wait()
                w_mate(j).wait_recv()
                w_relay(j).wait_recv()
        if 0 <= step - 2 < chunks:
            project(step - 2)
        if 0 <= step - 3 < chunks:
            convolve(step - 3)
        if 0 <= step - 5 < chunks:
            mix(step - 5)

    for d in range(1, n_seq):
        f_copy(d).wait_send()
    for part in range(per_block):
        own_mate(part).wait_send()
        for r in range(n_seq):

            @pl.when(r != z)
            def _():
                for k in range(2):
                    z_copy(r, part, k).wait_send()

    mate_w_in.wait_send()
    for j in range(2):
        w_x(j).wait_send()
        w_mate(j).wait_send()
        w_relay(j).wait_send()
    for i in range(chunks):
        b, part = divmod(i, per_block)

        @pl.when(b == z)
        def _():
            for k in range(2):
                own_x(part, k).wait_send()
            o_mate(i, b).wait_send()

        @pl.when(b != z)
        def _():
            x_copy(i).wait_send()
            for j in range(2):
                o_copy(i, j, b).wait_send()

        p_copy(i).wait_send()
        for k in range(2):
            g_copy(i, k).wait_send()
        g_mate(i).wait_send()
    for r in range(n_seq):
        held = out_ref.at[r]
        remote(held, held, o_send.at[0, 0], o_recv.at[r], chan=core_mate).wait_recv()


def by_record(n_seq, n_chan, records, norm_gain, in_projection, short_kernel, long_filter, skip_gain, out_projection):
    _, block_len, width = records.shape
    length = n_seq * block_len
    filters = long_filter.shape[0]
    chunks, half, per_block = length // width, width // 2, block_len // width
    hbm = pl.BlockSpec(memory_space=pltpu.HBM)
    dma = pltpu.SemaphoreType.DMA
    halves = pltpu.VMEM((chunks, n_chan, half, width), jnp.bfloat16)
    return pl.pallas_call(
        functools.partial(layer_kernel, n_seq, n_chan),
        out_shape=jax.ShapeDtypeStruct(records.shape, jnp.bfloat16),
        in_specs=[hbm] * 7,
        out_specs=hbm,
        scratch_shapes=[
            pltpu.VMEM((1, n_chan * width), jnp.float32),
            pltpu.VMEM((2, 3, n_chan * width, width), jnp.bfloat16),
            pltpu.VMEM((3, 3, width), jnp.float32),
            pltpu.VMEM((1, width), jnp.float32),
            halves,
            pltpu.VMEM((chunks, half, 3 * width), jnp.bfloat16),
            pltpu.VMEM((chunks, half, 3 * width), jnp.bfloat16),
            pltpu.VMEM((8 + length, 3 * width), jnp.float32),
            pltpu.VMEM((n_seq, filters, block_len), jnp.bfloat16),
            pltpu.VMEM((filters * width, length), jnp.bfloat16),
            pltpu.VMEM((length, width), jnp.bfloat16),
            pltpu.VMEM((chunks, 2, half, width), jnp.bfloat16),
            halves,
            pltpu.VMEM((2, n_chan * width, width), jnp.bfloat16),
            pltpu.VMEM((chunks, 2, half, width), jnp.bfloat16),
            dma((n_seq, per_block, 2)),
            dma((chunks,)),
            dma((chunks, 2)),
            dma((chunks,)),
            dma((per_block,)),
            dma((chunks,)),
            dma((chunks,)),
            dma((chunks, 3)),
            dma((chunks,)),
            dma((chunks, 2)),
            dma((n_seq,)),
            dma((n_seq,)),
            dma((n_seq,)),
            dma((8,)),
            dma((8,)),
            dma((8,)),
        ],
        compiler_params=pltpu.CompilerParams(
            collective_id=0, has_side_effects=True, vmem_limit_bytes=63 * 1024 * 1024
        ),
    )(
        records,
        norm_gain[None, :],
        in_projection.transpose(1, 0, 2),
        short_kernel,
        long_filter,
        skip_gain[None, :],
        out_projection,
    )


def solution(mesh):
    placed = (
        P("parts", "seq", "chan"),
        P(),
        P(None, None, "chan"),
        P(None, None, "chan"),
        P("chan", "seq"),
        P("chan"),
        P("chan", None),
    )
    n_seq, n_chan, n_parts = mesh.shape["seq"], mesh.shape["chan"], mesh.shape["parts"]

    def apply(*args):
        records = args[0]
        block_len, width = records.shape[1] // n_seq, records.shape[2] // n_chan
        whole_records = records.shape[0] // n_parts == n_seq
        if whole_records and n_chan == 4 and width == 128 and block_len % width == 0:
            chosen = functools.partial(by_record, n_seq, n_chan)
        else:
            chosen = body
        return jax.shard_map(
            chosen, mesh=mesh, in_specs=placed, out_specs=P("parts", "seq", "chan"), check_vma=False
        )(*args)

    return apply
```

```python
import functools

import jax
import jax.numpy as jnp
from jax import lax
from jax.experimental import pallas as pl
from jax.experimental.pallas import tpu as pltpu
from jax.sharding import PartitionSpec as P


def from_behind(block, axis, distance):
    devices = range(lax.axis_size(axis))
    route = [(i - distance, i) for i in devices if i - distance in devices]
    return lax.ppermute(block, axis, route)


def block_terms(taps_padded, offset, block_source, block_len):
    filter_count = taps_padded.shape[0]
    window = lax.dynamic_slice_in_dim(taps_padded, offset + 1, 2 * block_len - 1, 1)
    flipped = window[:, ::-1]
    padded = jnp.pad(flipped, ((0, 0), (0, 1)))
    tiled_taps = jnp.tile(padded, (1, block_len))
    toeplitz = tiled_taps[:, block_len - 1 : block_len - 1 + block_len * (2 * block_len - 1)]
    toeplitz = toeplitz.reshape(filter_count, block_len, 2 * block_len - 1)[:, :, :block_len]
    record_count = block_source.shape[0]
    grouped = block_source.reshape(record_count, block_len, filter_count, -1)
    return jnp.einsum("fab,rbfg->rafg", toeplitz, grouped, preferred_element_type=jnp.float32)


def body(records, norm_gain, in_projection, short_kernel, long_filter, skip_gain, out_projection):
    gathered = lax.all_gather(records, "chan", axis=2, tiled=True)
    widened = gathered.astype(jnp.float32)
    inv_rms = lax.rsqrt(jnp.mean(widened * widened, axis=-1, keepdims=True) + 1e-06)
    normed = (widened * inv_rms * norm_gain).astype(jnp.bfloat16)
    projected = jnp.einsum(
        "rtd,dkc->rtkc", normed, in_projection, preferred_element_type=jnp.float32
    ).astype(jnp.bfloat16)
    rim_rows = from_behind(projected[:, -2:], "seq", 1)
    extended = jnp.concatenate([rim_rows, projected], axis=1).astype(jnp.float32)
    streams = (
        short_kernel[0] * extended[:, 2:]
        + short_kernel[1] * extended[:, 1:-1]
        + short_kernel[2] * extended[:, :-2]
    )
    query_gate = streams[:, :, 0]
    gated_source = (streams[:, :, 1] * streams[:, :, 2]).astype(jnp.bfloat16)
    record_count = gated_source.shape[0]
    block_len = gated_source.shape[1]
    channels = gated_source.shape[2]
    all_taps = lax.all_gather(long_filter, "seq", axis=1, tiled=True)
    taps_padded = jnp.concatenate(
        [jnp.zeros((all_taps.shape[0], block_len), jnp.bfloat16), all_taps], axis=1
    )
    my_start = lax.axis_index("seq") * block_len
    cycle_stops = lax.axis_size("seq")
    long_sum = block_terms(taps_padded, 0, gated_source, block_len)

    def advance(stop_index, state):
        running_sum, visiting = state
        visiting = from_behind(visiting, "seq", 1)
        lag_start = stop_index * block_len
        running_sum = lax.cond(
            lag_start <= my_start,
            lambda running: running + block_terms(taps_padded, lag_start, visiting, block_len),
            lambda running: running,
            running_sum,
        )
        return (running_sum, visiting)

    long_sum, visiting = lax.fori_loop(1, cycle_stops, advance, (long_sum, gated_source))
    long_out = long_sum.reshape(
        record_count, block_len, channels
    ) + skip_gain * gated_source.astype(jnp.float32)
    gated = (query_gate * long_out).astype(jnp.bfloat16)
    partial_terms = jnp.einsum(
        "rtc,cd->rtd", gated, out_projection, preferred_element_type=jnp.float32
    )
    return lax.psum_scatter(
        partial_terms.astype(jnp.bfloat16), "chan", scatter_dimension=2, tiled=True
    )


MESH = pl.DeviceIdType.MESH
GIVES = (
    ((1, 0), (2, 0), (3, 0), (1, 1), (2, 1), (3, 1), (1, 2), (2, 2), (3, 2)),
    ((0, 0), (2, 0), (3, 0), (0, 1), (2, 1), (3, 1), (0, 2), (2, 2), (3, 2)),
    ((0, 0), (1, 0), (3, 0), (0, 1), (1, 1), (3, 1), (0, 2), (1, 2), (3, 2)),
    ((2, 0), (2, 1), (2, 2), (1, 0), (0, 0), (1, 1), (0, 1), (1, 2), (0, 2)),
)
STEPS = (
    ((0, 3), (1, 0), (0, 6), (1, 1), (2, 0), (0, 4), (1, 2), (2, 1), (0, 7), (2, 2), (0, 5), (0, 8), (1, 3),
     (0, 9), (1, 6), (2, 3), (3, 0), (1, 4), (0, 10), (3, 1), (2, 4), (1, 7), (0, 11), (3, 2), (1, 5), (1, 8),
     (2, 6), (2, 7), (2, 8), (3, 3), (2, 5), (1, 9), (1, 10), (3, 4), (2, 9), (2, 10), (1, 11), (3, 6), (2, 11),
     (3, 7), (3, 8), (3, 5), (3, 9), (3, 10), (3, 11)),
    ((1, 3), (1, 4), (0, 0), (0, 6), (1, 5), (0, 7), (0, 9), (0, 1), (1, 0), (1, 6), (2, 0), (1, 7), (0, 2),
     (0, 8), (1, 9), (0, 10), (1, 1), (3, 0), (0, 11), (2, 1), (1, 2), (1, 8), (2, 2), (2, 6), (2, 7), (2, 9),
     (2, 8), (3, 1), (2, 3), (2, 4), (2, 5), (3, 2), (1, 10), (3, 6), (1, 11), (3, 7), (2, 10), (2, 11), (3, 9),
     (3, 8), (3, 3), (3, 4), (3, 5), (3, 10), (3, 11)),
    ((1, 6), (0, 9), (0, 3), (1, 7), (0, 10), (1, 8), (0, 11), (0, 4), (0, 0), (1, 9), (1, 3), (0, 5), (1, 10),
     (0, 1), (1, 11), (1, 4), (1, 0), (0, 2), (1, 5), (2, 0), (1, 1), (1, 2), (2, 1), (3, 0), (2, 2), (2, 3),
     (2, 4), (2, 5), (3, 1), (2, 9), (2, 10), (3, 2), (2, 11), (3, 3), (2, 6), (2, 7), (3, 4), (2, 8), (3, 5),
     (3, 9), (3, 10), (3, 11), (3, 6), (3, 7), (3, 8)),
    ((1, 9), (0, 6), (1, 10), (0, 7), (1, 11), (0, 8), (0, 3), (1, 6), (0, 4), (1, 7), (0, 0), (1, 8), (1, 3),
     (1, 4), (0, 5), (1, 0), (0, 1), (2, 0), (1, 5), (0, 2), (1, 1), (3, 0), (2, 1), (1, 2), (2, 2), (2, 3),
     (3, 1), (2, 4), (2, 5), (2, 6), (2, 7), (3, 2), (2, 8), (2, 9), (3, 3), (2, 10), (3, 4), (2, 11), (3, 5),
     (3, 6), (3, 7), (3, 8), (3, 9), (3, 10), (3, 11)),
)


def when(condition):
    def run(act):
        if condition:
            act()

    return run


def layer_kernel(
    n_seq, n_chan, recs_ref, gain_hbm, w_in_hbm, short_hbm, taps_ref, skip_hbm, w_out_ref, out_ref,
    gain_ref, w_in_ref, short_ref, skip_ref, first, stage, peer, proj, taps, strips, query, source, gated, second,
    w_out, mixed, z_recv, x_recv, p_recv, g_recv, here_sem, sent, got,
):
    z = lax.axis_index("seq")
    c = lax.axis_index("chan")
    barrier = pltpu.get_barrier_semaphore()
    for d in range(1, n_seq):
        for k in range(2):
            pl.semaphore_signal(
                barrier, inc=1, device_id={"seq": (z + d) % n_seq, "chan": c - c % 2 + k}, device_id_type=MESH
            )
    for d in range(1, n_chan):
        pl.semaphore_signal(barrier, inc=1, device_id={"chan": (c + d) % n_chan}, device_id_type=MESH)
    pl.semaphore_wait(barrier, 2 * (n_seq - 1) + n_chan - 1)
    for q in range(n_seq):

        @pl.when(z == q)
        def _():
            program(
                n_seq, n_chan, q, recs_ref, gain_hbm, w_in_hbm, short_hbm, taps_ref, skip_hbm, w_out_ref, out_ref,
                gain_ref, w_in_ref, short_ref, skip_ref, first, stage, peer, proj, taps, strips, query, source,
                gated, second, w_out, mixed, z_recv, x_recv, p_recv, g_recv, here_sem, sent, got,
            )


def program(
    n_seq, n_chan, z, recs_ref, gain_hbm, w_in_hbm, short_hbm, taps_ref, skip_hbm, w_out_ref, out_ref,
    gain_ref, w_in_ref, short_ref, skip_ref, first, stage, peer, proj, taps, strips, query, source,
    gated, second, w_out, mixed, z_recv, x_recv, p_recv, g_recv, here_sem, sent, got,
):
    block_len, width = recs_ref.shape[1], recs_ref.shape[2]
    length = n_seq * block_len
    filters = taps_ref.shape[0]
    group = width // filters
    half = width // 2
    per_block = block_len // width
    chunks = n_seq * per_block
    c = lax.axis_index("chan")
    core = c % 2
    here = c - core
    there = (here + n_chan // 2) % n_chan
    core_mate = here + 1 - core
    chip_mate = there + core

    def remote(src, dst, send, recv, **device):
        return pltpu.make_async_remote_copy(
            src_ref=src, dst_ref=dst, send_sem=send, recv_sem=recv, device_id=device, device_id_type=MESH
        )

    def rows(part, k):
        return pl.ds(pl.multiple_of(part * width + k * half, half), half)

    def f_copy(d):
        return remote(taps_ref, taps.at[z], sent.at[0], got.at[0], seq=(z + d) % n_seq)

    def z_copy(r, part, k):
        return remote(
            recs_ref.at[r, rows(part, k)], first.at[z * per_block + part, c],
            sent.at[1], z_recv.at[z * per_block + part], seq=r, chan=here + k,
        )

    def own_local(part):
        i = z * per_block + part
        return pltpu.make_async_copy(recs_ref.at[z, rows(part, core)], first.at[i, c], z_recv.at[i])

    def own_mate(part):
        i = z * per_block + part
        return remote(
            recs_ref.at[z, rows(part, 1 - core)], first.at[i, c], sent.at[2], z_recv.at[i], chan=core_mate
        )

    def own_x(part, k):
        i = z * per_block + part
        return remote(
            recs_ref.at[z, rows(part, k)], first.at[i, c], sent.at[3], x_recv.at[i], chan=there + k
        )

    def x_copy(i):
        held = first.at[i, pl.ds(here, 2)]
        return remote(held, held, sent.at[3], x_recv.at[i], chan=chip_mate)

    def z_wait(i):
        held = first.at[i, pl.ds(here, 2)]
        remote(held, held, sent.at[3], z_recv.at[i], chan=chip_mate).wait_recv()

    def x_wait(i):
        held = first.at[i, pl.ds(there, 2)]
        remote(held, held, sent.at[3], x_recv.at[i], chan=chip_mate).wait_recv()

    def p_copy(i):
        return remote(stage.at[i], peer.at[i], sent.at[4], p_recv.at[i], chan=core_mate)

    def g_copy(i, k):
        return remote(gated.at[i, k], second.at[i, c], sent.at[5], g_recv.at[i], chan=there + k)

    def g_mate(i):
        return remote(gated.at[i, 1 - core], second.at[i, c], sent.at[5], g_recv.at[i], chan=core_mate)

    def g_wait(i):
        held = second.at[i, pl.ds(0, 3)]
        remote(held, held, sent.at[5], g_recv.at[i], chan=core_mate).wait_recv()

    def o_copy(i, j, b):
        part = i - b * per_block
        return remote(
            mixed.at[i, j], out_ref.at[z, rows(part, core)], sent.at[6], got.at[1],
            seq=b, chan=core_mate if j else c,
        )

    def o_mate(i, b):
        part = i - b * per_block
        return remote(
            mixed.at[i, 1], out_ref.at[z, rows(part, core)], sent.at[7], got.at[1], chan=core_mate
        )

    def o_local(i, b):
        part = i - b * per_block
        return pltpu.make_async_copy(mixed.at[i, 0], out_ref.at[z, rows(part, core)], got.at[1])

    def columns(q):
        return pl.ds(pl.multiple_of(q * width, width), width)

    def w_x(j):
        owner = chip_mate if j == 0 else there + 1 - core
        return remote(
            w_out_ref.at[:, columns(owner)], w_out.at[j, columns(c)], sent.at[8], got.at[2], chan=chip_mate
        )

    def w_mate(j):
        owner = core_mate if j == 0 else c
        return remote(
            w_out_ref.at[:, columns(owner)], w_out.at[j, columns(c)],
            sent.at[8], got.at[3], chan=core_mate,
        )

    def w_relay(j):
        return remote(
            w_out.at[1 - j, columns(chip_mate)], w_out.at[j, columns(chip_mate)],
            sent.at[8], got.at[3], chan=core_mate,
        )

    def w_local(j):
        owner = c if j == 0 else core_mate
        return pltpu.make_async_copy(w_out_ref.at[:, columns(owner)], w_out.at[j, columns(c)], got.at[3])

    own_taps = pltpu.make_async_copy(taps_ref, taps.at[z], here_sem.at[2])
    own_w_in = pltpu.make_async_copy(w_in_hbm, w_in_ref.at[0], got.at[4])
    mate_w_in = remote(w_in_hbm, w_in_ref.at[1], sent.at[9], got.at[4], chan=core_mate)
    fetched = [
        pltpu.make_async_copy(src, dst, here_sem.at[4 + j])
        for j, (src, dst) in enumerate([(gain_hbm, gain_ref), (short_hbm, short_ref), (skip_hbm, skip_ref)])
    ]

    def done(ref, sem):
        remote(ref, ref, sem, got.at[0], chan=core_mate).wait_send()

    def arrived(ref, sem):
        remote(ref, ref, sent.at[0], sem, chan=core_mate).wait_recv()

    for d in range(1, n_seq):
        f_copy(d).start()
    for part in range(per_block):
        for k in range(2):
            own_x(part, k).start()
    for r, part in GIVES[z]:
        for k in range(2):
            z_copy(r, part, k).start()

    for part in range(per_block):
        own_local(part).start()
        own_mate(part).start()
    own_taps.start()
    own_w_in.start()
    mate_w_in.start()
    for copy in fetched:
        copy.start()
    for j in range(2):
        w_x(j).start()
        w_mate(j).start()
        w_local(j).start()

    def build_strips():
        own_taps.wait()
        arrived(taps.at[pl.ds(0, n_seq - 1)], got.at[0])
        rows = lax.broadcasted_iota(jnp.int32, (width, width), 0)
        columns = lax.broadcasted_iota(jnp.int32, (width, width), 1)
        mirror = jnp.where(rows + columns == width - 1, 1.0, 0.0).astype(jnp.bfloat16)
        pieces = []
        for s in reversed(range(n_seq)):
            held = taps[s]
            for j in reversed(range(block_len // width)):
                pieces.append(
                    jnp.dot(held[:, j * width : (j + 1) * width], mirror, preferred_element_type=jnp.float32)
                )
        pieces.append(jnp.zeros((filters, width), jnp.float32))
        backward = jnp.concatenate(pieces, axis=1)
        for f in range(filters):
            row = jnp.broadcast_to(backward[f : f + 1], (width, length + width))
            turned = pltpu.roll(row, 1, 1, stride=1, stride_axis=0)
            strips[f * width : (f + 1) * width, :] = turned[:, width:].astype(jnp.bfloat16)

    def proj_rows(i, k):
        return pl.ds(pl.multiple_of(8 + i * width + k * half, 8), half)

    def spread(i):
        z_wait(i)
        x_copy(i).start()

    def project(i):
        if i // per_block == z:
            z_wait(i)
        x_wait(i)
        wide = jnp.concatenate([first[i, q] for q in range(n_chan)], axis=1).astype(jnp.float32)
        inv_rms = lax.rsqrt(jnp.mean(wide * wide, axis=-1, keepdims=True) + 1e-06)
        normed = (wide * inv_rms * gain_ref[...]).astype(jnp.bfloat16)
        weights = jnp.concatenate([w_in_ref[j, k] for j in range(2) for k in range(3)], axis=1)
        got = jnp.dot(normed, weights, preferred_element_type=jnp.float32).astype(jnp.bfloat16)
        stage[i] = got[:, 3 * width :]
        p_copy(i).start()
        proj[proj_rows(i, core), :] = got[:, : 3 * width].astype(jnp.float32)

    formed = set()

    def form(i):
        if i in formed:
            return
        formed.add(i)
        p_copy(i).wait_recv()
        proj[proj_rows(i, 1 - core), :] = peer[i].astype(jnp.float32)
        if i > 0:
            form(i - 1)
        short = [jnp.concatenate([short_ref[j, k : k + 1] for k in range(3)], axis=1) for j in range(3)]
        now = proj[8 + i * width : 8 + (i + 1) * width, :]
        back1 = proj[7 + i * width : 7 + (i + 1) * width, :]
        back2 = proj[6 + i * width : 6 + (i + 1) * width, :]
        streams = short[0] * now + short[1] * back1 + short[2] * back2
        query[i] = streams[:, 0:width]
        source[i * width : (i + 1) * width, :] = (
            streams[:, width : 2 * width] * streams[:, 2 * width :]
        ).astype(jnp.bfloat16)

    def convolve(i):
        form(i)
        lane_group = lax.broadcasted_iota(jnp.int32, (width, width), 1) // group
        depth = (i + 1) * width
        sums = jnp.dot(strips[:, length - depth :], source[0:depth, :], preferred_element_type=jnp.float32)
        total = sums[0:width]
        for f in range(1, filters):
            total = jnp.where(lane_group == f, sums[f * width : (f + 1) * width], total)
        total = total + skip_ref[...] * source[i * width : (i + 1) * width, :].astype(jnp.float32)
        result = (query[i] * total).astype(jnp.bfloat16)
        for k in range(2):
            gated[i, k] = result[k * half : (k + 1) * half]
        for k in range(2):
            g_copy(i, k).start()
        g_mate(i).start()
        second[i, c] = gated[i, core]

    def mix(i):
        b = i // per_block
        g_wait(i)
        wide = jnp.concatenate([second[i, q] for q in range(n_chan)], axis=1)
        weights = jnp.concatenate([w_out[0], w_out[1]], axis=1)
        got = jnp.dot(wide, weights, preferred_element_type=jnp.float32).astype(jnp.bfloat16)
        for j in range(2):
            mixed[i, j] = got[:, j * width : (j + 1) * width]

        @when(b == z)
        def _():
            o_local(i, b).start()
            o_mate(i, b).start()

        @when(b != z)
        def _():
            for j in range(2):
                o_copy(i, j, b).start()

    proj[0:8, :] = jnp.zeros((8, proj.shape[1]), jnp.float32)
    seen = [0, 0, 0, 0]
    relayed = False
    for kind, i in STEPS[z]:
        if kind == 1 and seen[1] == 0:
            arrived(w_in_ref, got.at[4])
            for copy in fetched:
                copy.wait()
        if kind == 2 and seen[2] == 0:
            build_strips()
        if not relayed and (kind == 2 and seen[2] == 1 or kind == 3):
            relayed = True
            arrived(w_out.at[:, pl.ds(0, width)], got.at[2])
            for j in range(2):
                w_relay(j).start()
        if kind == 3 and seen[3] == 0:
            arrived(first.at[pl.ds(0, 3)], got.at[3])
        (spread, project, convolve, mix)[kind](i)
        seen[kind] += 1

    done(taps.at[pl.ds(0, n_seq - 1)], sent.at[0])
    done(recs_ref.at[pl.ds(0, n_seq - 1)], sent.at[1])
    done(recs_ref.at[0, pl.ds(0, block_len // 2)], sent.at[2])
    done(recs_ref, sent.at[3])
    done(stage, sent.at[4])
    done(second.at[pl.ds(0, 3 * per_block)], sent.at[5])
    done(recs_ref.at[pl.ds(0, n_seq - 1)], sent.at[6])
    done(recs_ref.at[0, pl.ds(0, block_len // 2)], sent.at[7])
    done(first.at[pl.ds(0, 3)], sent.at[8])
    done(w_in_hbm, sent.at[9])
    arrived(out_ref, got.at[1])


def by_record(n_seq, n_chan, records, norm_gain, in_projection, short_kernel, long_filter, skip_gain, out_projection):
    _, block_len, width = records.shape
    length = n_seq * block_len
    filters = long_filter.shape[0]
    chunks, half, per_block = length // width, width // 2, block_len // width
    hbm = pl.BlockSpec(memory_space=pltpu.HBM)
    dma = pltpu.SemaphoreType.DMA
    halves = pltpu.VMEM((chunks, n_chan, half, width), jnp.bfloat16)
    return pl.pallas_call(
        functools.partial(layer_kernel, n_seq, n_chan),
        out_shape=jax.ShapeDtypeStruct(records.shape, jnp.bfloat16),
        in_specs=[hbm] * 7,
        out_specs=hbm,
        scratch_shapes=[
            pltpu.VMEM((1, n_chan * width), jnp.float32),
            pltpu.VMEM((2, 3, n_chan * width, width), jnp.bfloat16),
            pltpu.VMEM((3, 3, width), jnp.float32),
            pltpu.VMEM((1, width), jnp.float32),
            halves,
            pltpu.VMEM((chunks, half, 3 * width), jnp.bfloat16),
            pltpu.VMEM((chunks, half, 3 * width), jnp.bfloat16),
            pltpu.VMEM((8 + length, 3 * width), jnp.float32),
            pltpu.VMEM((n_seq, filters, block_len), jnp.bfloat16),
            pltpu.VMEM((filters * width, length), jnp.bfloat16),
            pltpu.VMEM((chunks, width, width), jnp.float32),
            pltpu.VMEM((length, width), jnp.bfloat16),
            pltpu.VMEM((chunks, 2, half, width), jnp.bfloat16),
            halves,
            pltpu.VMEM((2, n_chan * width, width), jnp.bfloat16),
            pltpu.VMEM((chunks, 2, half, width), jnp.bfloat16),
            dma((chunks,)),
            dma((chunks,)),
            dma((chunks,)),
            dma((chunks,)),
            dma((8,)),
            dma((10,)),
            dma((5,)),
        ],
        compiler_params=pltpu.CompilerParams(
            collective_id=0, has_side_effects=True, vmem_limit_bytes=40 * 1024 * 1024
        ),
    )(
        *(
            pltpu.with_memory_space_constraint(value, pltpu.HBM)
            for value in (
                records,
                norm_gain[None, :],
                in_projection.transpose(1, 0, 2),
                short_kernel,
                long_filter,
                skip_gain[None, :],
                out_projection,
            )
        )
    )


def solution(mesh):
    placed = (
        P("parts", "seq", "chan"),
        P(),
        P(None, None, "chan"),
        P(None, None, "chan"),
        P("chan", "seq"),
        P("chan"),
        P("chan", None),
    )
    n_seq, n_chan, n_parts = mesh.shape["seq"], mesh.shape["chan"], mesh.shape["parts"]

    def apply(*args):
        records = args[0]
        block_len, width = records.shape[1] // n_seq, records.shape[2] // n_chan
        whole_records = records.shape[0] // n_parts == n_seq
        if whole_records and n_seq == 4 and n_chan == 4 and width == 128 and block_len % width == 0:
            chosen = functools.partial(by_record, n_seq, n_chan)
        else:
            chosen = body
        return jax.shard_map(
            chosen, mesh=mesh, in_specs=placed, out_specs=P("parts", "seq", "chan"), check_vma=False
        )(*args)

    return apply
```

```python
import functools

import jax
import jax.numpy as jnp
from jax import lax
from jax.experimental import pallas as pl
from jax.experimental.pallas import tpu as pltpu
from jax.sharding import PartitionSpec as P


def from_behind(block, axis, distance):
    devices = range(lax.axis_size(axis))
    route = [(i - distance, i) for i in devices if i - distance in devices]
    return lax.ppermute(block, axis, route)


def block_terms(taps_padded, offset, block_source, block_len):
    filter_count = taps_padded.shape[0]
    window = lax.dynamic_slice_in_dim(taps_padded, offset + 1, 2 * block_len - 1, 1)
    flipped = window[:, ::-1]
    padded = jnp.pad(flipped, ((0, 0), (0, 1)))
    tiled_taps = jnp.tile(padded, (1, block_len))
    toeplitz = tiled_taps[:, block_len - 1 : block_len - 1 + block_len * (2 * block_len - 1)]
    toeplitz = toeplitz.reshape(filter_count, block_len, 2 * block_len - 1)[:, :, :block_len]
    record_count = block_source.shape[0]
    grouped = block_source.reshape(record_count, block_len, filter_count, -1)
    return jnp.einsum("fab,rbfg->rafg", toeplitz, grouped, preferred_element_type=jnp.float32)


def body(records, norm_gain, in_projection, short_kernel, long_filter, skip_gain, out_projection):
    gathered = lax.all_gather(records, "chan", axis=2, tiled=True)
    widened = gathered.astype(jnp.float32)
    inv_rms = lax.rsqrt(jnp.mean(widened * widened, axis=-1, keepdims=True) + 1e-06)
    normed = (widened * inv_rms * norm_gain).astype(jnp.bfloat16)
    projected = jnp.einsum(
        "rtd,dkc->rtkc", normed, in_projection, preferred_element_type=jnp.float32
    ).astype(jnp.bfloat16)
    rim_rows = from_behind(projected[:, -2:], "seq", 1)
    extended = jnp.concatenate([rim_rows, projected], axis=1).astype(jnp.float32)
    streams = (
        short_kernel[0] * extended[:, 2:]
        + short_kernel[1] * extended[:, 1:-1]
        + short_kernel[2] * extended[:, :-2]
    )
    query_gate = streams[:, :, 0]
    gated_source = (streams[:, :, 1] * streams[:, :, 2]).astype(jnp.bfloat16)
    record_count = gated_source.shape[0]
    block_len = gated_source.shape[1]
    channels = gated_source.shape[2]
    all_taps = lax.all_gather(long_filter, "seq", axis=1, tiled=True)
    taps_padded = jnp.concatenate(
        [jnp.zeros((all_taps.shape[0], block_len), jnp.bfloat16), all_taps], axis=1
    )
    my_start = lax.axis_index("seq") * block_len
    cycle_stops = lax.axis_size("seq")
    long_sum = block_terms(taps_padded, 0, gated_source, block_len)

    def advance(stop_index, state):
        running_sum, visiting = state
        visiting = from_behind(visiting, "seq", 1)
        lag_start = stop_index * block_len
        running_sum = lax.cond(
            lag_start <= my_start,
            lambda running: running + block_terms(taps_padded, lag_start, visiting, block_len),
            lambda running: running,
            running_sum,
        )
        return (running_sum, visiting)

    long_sum, visiting = lax.fori_loop(1, cycle_stops, advance, (long_sum, gated_source))
    long_out = long_sum.reshape(
        record_count, block_len, channels
    ) + skip_gain * gated_source.astype(jnp.float32)
    gated = (query_gate * long_out).astype(jnp.bfloat16)
    partial_terms = jnp.einsum(
        "rtc,cd->rtd", gated, out_projection, preferred_element_type=jnp.float32
    )
    return lax.psum_scatter(
        partial_terms.astype(jnp.bfloat16), "chan", scatter_dimension=2, tiled=True
    )


MESH = pl.DeviceIdType.MESH
GIVES = (
    ((1, 0), (2, 0), (3, 0), (1, 1), (2, 1), (3, 1), (1, 2), (2, 2), (3, 2)),
    ((0, 0), (2, 0), (3, 0), (0, 1), (2, 1), (3, 1), (0, 2), (2, 2), (3, 2)),
    ((0, 0), (1, 0), (3, 0), (0, 1), (1, 1), (3, 1), (0, 2), (1, 2), (3, 2)),
    ((2, 0), (2, 1), (2, 2), (1, 0), (0, 0), (1, 1), (0, 1), (1, 2), (0, 2)),
)
STEPS = (
    ((0, 3), (1, 0), (0, 6), (1, 1), (2, 0), (0, 4), (1, 2), (2, 1), (0, 7), (2, 2), (0, 5), (0, 8), (1, 3),
     (0, 9), (1, 6), (2, 3), (3, 0), (1, 4), (0, 10), (3, 1), (2, 4), (1, 7), (0, 11), (3, 2), (1, 5), (1, 8),
     (2, 6), (2, 7), (2, 8), (3, 3), (2, 5), (1, 9), (1, 10), (3, 4), (2, 9), (2, 10), (1, 11), (3, 6), (2, 11),
     (3, 7), (3, 8), (3, 5), (3, 9), (3, 10), (3, 11)),
    ((1, 3), (1, 4), (0, 0), (0, 6), (1, 5), (0, 7), (0, 9), (0, 1), (1, 0), (1, 6), (2, 0), (1, 7), (0, 2),
     (0, 8), (1, 9), (0, 10), (1, 1), (3, 0), (0, 11), (2, 1), (1, 2), (1, 8), (2, 2), (2, 6), (2, 7), (2, 9),
     (2, 8), (3, 1), (2, 3), (2, 4), (2, 5), (3, 2), (1, 10), (3, 6), (1, 11), (3, 7), (2, 10), (2, 11), (3, 9),
     (3, 8), (3, 3), (3, 4), (3, 5), (3, 10), (3, 11)),
    ((1, 6), (0, 9), (0, 3), (1, 7), (0, 10), (1, 8), (0, 11), (0, 4), (0, 0), (1, 9), (1, 3), (0, 5), (1, 10),
     (0, 1), (1, 11), (1, 4), (1, 0), (0, 2), (1, 5), (2, 0), (1, 1), (1, 2), (2, 1), (3, 0), (2, 2), (2, 3),
     (2, 4), (2, 5), (3, 1), (2, 9), (2, 10), (3, 2), (2, 11), (3, 3), (2, 6), (2, 7), (3, 4), (2, 8), (3, 5),
     (3, 9), (3, 10), (3, 11), (3, 6), (3, 7), (3, 8)),
    ((1, 9), (0, 6), (1, 10), (0, 7), (1, 11), (0, 8), (0, 3), (1, 6), (0, 4), (1, 7), (0, 0), (1, 8), (1, 3),
     (1, 4), (0, 5), (1, 0), (0, 1), (2, 0), (1, 5), (0, 2), (1, 1), (3, 0), (2, 1), (1, 2), (2, 2), (2, 3),
     (3, 1), (2, 4), (2, 5), (2, 6), (2, 7), (3, 2), (2, 8), (2, 9), (3, 3), (2, 10), (3, 4), (2, 11), (3, 5),
     (3, 6), (3, 7), (3, 8), (3, 9), (3, 10), (3, 11)),
)


def when(condition):
    def run(act):
        if condition:
            act()

    return run


def layer_kernel(
    n_seq, n_chan, recs_ref, gain_hbm, w_in_hbm, short_hbm, taps_ref, skip_hbm, w_out_ref, out_ref,
    gain_ref, w_in_ref, short_ref, skip_ref, first, stage, peer, proj, taps, strips, query, source, gated, second,
    w_out, mixed, z_recv, x_recv, p_recv, g_recv, here_sem, sent, got,
):
    z = lax.axis_index("seq")
    c = lax.axis_index("chan")
    barrier = pltpu.get_barrier_semaphore()
    for d in range(1, n_seq):
        for k in range(2):
            pl.semaphore_signal(
                barrier, inc=1, device_id={"seq": (z + d) % n_seq, "chan": c - c % 2 + k}, device_id_type=MESH
            )
    for d in range(1, n_chan):
        pl.semaphore_signal(barrier, inc=1, device_id={"chan": (c + d) % n_chan}, device_id_type=MESH)
    pl.semaphore_wait(barrier, 2 * (n_seq - 1) + n_chan - 1)
    for q in range(n_seq):

        @pl.when(z == q)
        def _():
            program(
                n_seq, n_chan, q, recs_ref, gain_hbm, w_in_hbm, short_hbm, taps_ref, skip_hbm, w_out_ref, out_ref,
                gain_ref, w_in_ref, short_ref, skip_ref, first, stage, peer, proj, taps, strips, query, source,
                gated, second, w_out, mixed, z_recv, x_recv, p_recv, g_recv, here_sem, sent, got,
            )


def program(
    n_seq, n_chan, z, recs_ref, gain_hbm, w_in_hbm, short_hbm, taps_ref, skip_hbm, w_out_ref, out_ref,
    gain_ref, w_in_ref, short_ref, skip_ref, first, stage, peer, proj, taps, strips, query, source,
    gated, second, w_out, mixed, z_recv, x_recv, p_recv, g_recv, here_sem, sent, got,
):
    block_len, width = recs_ref.shape[1], recs_ref.shape[2]
    length = n_seq * block_len
    filters = taps_ref.shape[0]
    group = width // filters
    half = width // 2
    per_block = block_len // width
    chunks = n_seq * per_block
    c = lax.axis_index("chan")
    core = c % 2
    here = c - core
    there = (here + n_chan // 2) % n_chan
    core_mate = here + 1 - core
    chip_mate = there + core

    def remote(src, dst, send, recv, **device):
        return pltpu.make_async_remote_copy(
            src_ref=src, dst_ref=dst, send_sem=send, recv_sem=recv, device_id=device, device_id_type=MESH
        )

    def rows(part, k):
        return pl.ds(pl.multiple_of(part * width + k * half, half), half)

    def f_copy(d):
        return remote(taps_ref, taps.at[z], sent.at[0], got.at[0], seq=(z + d) % n_seq)

    def z_copy(r, part, k):
        return remote(
            recs_ref.at[r, rows(part, k)], first.at[z * per_block + part, c],
            sent.at[1], z_recv.at[z * per_block + part], seq=r, chan=here + k,
        )

    def own_local(part):
        i = z * per_block + part
        return pltpu.make_async_copy(recs_ref.at[z, rows(part, core)], first.at[i, c], z_recv.at[i])

    def own_mate(part):
        i = z * per_block + part
        return remote(
            recs_ref.at[z, rows(part, 1 - core)], first.at[i, c], sent.at[2], z_recv.at[i], chan=core_mate
        )

    def own_x(part, k):
        i = z * per_block + part
        return remote(
            recs_ref.at[z, rows(part, k)], first.at[i, c], sent.at[3], x_recv.at[i], chan=there + k
        )

    def x_copy(i):
        held = first.at[i, pl.ds(here, 2)]
        return remote(held, held, sent.at[3], x_recv.at[i], chan=chip_mate)

    def z_wait(i):
        held = first.at[i, pl.ds(here, 2)]
        remote(held, held, sent.at[3], z_recv.at[i], chan=chip_mate).wait_recv()

    def x_wait(i):
        held = first.at[i, pl.ds(there, 2)]
        remote(held, held, sent.at[3], x_recv.at[i], chan=chip_mate).wait_recv()

    def p_copy(i):
        return remote(stage.at[i], peer.at[i], sent.at[4], p_recv.at[i], chan=core_mate)

    def g_copy(i, k):
        return remote(gated.at[i, k], second.at[i, c], sent.at[5], g_recv.at[i], chan=there + k)

    def g_mate(i):
        return remote(gated.at[i, 1 - core], second.at[i, c], sent.at[5], g_recv.at[i], chan=core_mate)

    def g_wait(i):
        held = second.at[i, pl.ds(0, 3)]
        remote(held, held, sent.at[5], g_recv.at[i], chan=core_mate).wait_recv()

    def o_copy(i, j, b):
        part = i - b * per_block
        return remote(
            mixed.at[i, j], out_ref.at[z, rows(part, core)], sent.at[6], got.at[1],
            seq=b, chan=core_mate if j else c,
        )

    def o_mate(i, b):
        part = i - b * per_block
        return remote(
            mixed.at[i, 1], out_ref.at[z, rows(part, core)], sent.at[7], got.at[1], chan=core_mate
        )

    def o_local(i, b):
        part = i - b * per_block
        return pltpu.make_async_copy(mixed.at[i, 0], out_ref.at[z, rows(part, core)], got.at[1])

    def columns(q):
        return pl.ds(pl.multiple_of(q * width, width), width)

    def w_x(j):
        owner = chip_mate if j == 0 else there + 1 - core
        return remote(
            w_out_ref.at[:, columns(owner)], w_out.at[j, columns(c)], sent.at[8], got.at[2], chan=chip_mate
        )

    def w_mate(j):
        owner = core_mate if j == 0 else c
        return remote(
            w_out_ref.at[:, columns(owner)], w_out.at[j, columns(c)],
            sent.at[8], got.at[3], chan=core_mate,
        )

    def w_relay(j):
        return remote(
            w_out.at[1 - j, columns(chip_mate)], w_out.at[j, columns(chip_mate)],
            sent.at[8], got.at[3], chan=core_mate,
        )

    def w_local(j):
        owner = c if j == 0 else core_mate
        return pltpu.make_async_copy(w_out_ref.at[:, columns(owner)], w_out.at[j, columns(c)], got.at[3])

    own_taps = pltpu.make_async_copy(taps_ref, taps.at[z], here_sem.at[2])
    own_w_in = pltpu.make_async_copy(w_in_hbm, w_in_ref.at[0], got.at[4])
    mate_w_in = remote(w_in_hbm, w_in_ref.at[1], sent.at[9], got.at[4], chan=core_mate)
    fetched = [
        pltpu.make_async_copy(src, dst, here_sem.at[4 + j])
        for j, (src, dst) in enumerate([(gain_hbm, gain_ref), (short_hbm, short_ref), (skip_hbm, skip_ref)])
    ]

    def done(ref, sem):
        remote(ref, ref, sem, got.at[0], chan=core_mate).wait_send()

    def arrived(ref, sem):
        remote(ref, ref, sent.at[0], sem, chan=core_mate).wait_recv()

    for d in range(1, n_seq):
        f_copy(d).start()
    for part in range(per_block):
        for k in range(2):
            own_x(part, k).start()
    for r, part in GIVES[z]:
        for k in range(2):
            z_copy(r, part, k).start()

    for part in range(per_block):
        own_local(part).start()
        own_mate(part).start()
    own_taps.start()
    own_w_in.start()
    mate_w_in.start()
    for copy in fetched:
        copy.start()
    for j in range(2):
        w_x(j).start()
        w_mate(j).start()
        w_local(j).start()

    def build_strips():
        own_taps.wait()
        arrived(taps.at[pl.ds(0, n_seq - 1)], got.at[0])
        rows = lax.broadcasted_iota(jnp.int32, (width, width), 0)
        columns = lax.broadcasted_iota(jnp.int32, (width, width), 1)
        mirror = jnp.where(rows + columns == width - 1, 1.0, 0.0).astype(jnp.bfloat16)
        pieces = []
        for s in reversed(range(n_seq)):
            held = taps[s]
            for j in reversed(range(block_len // width)):
                pieces.append(
                    jnp.dot(held[:, j * width : (j + 1) * width], mirror, preferred_element_type=jnp.float32)
                )
        pieces.append(jnp.zeros((filters, width), jnp.float32))
        backward = jnp.concatenate(pieces, axis=1)
        for f in range(filters):
            row = jnp.broadcast_to(backward[f : f + 1], (width, length + width))
            turned = pltpu.roll(row, 1, 1, stride=1, stride_axis=0)
            strips[f * width : (f + 1) * width, :] = turned[:, width:].astype(jnp.bfloat16)

    def proj_rows(i, k):
        return pl.ds(pl.multiple_of(8 + i * width + k * half, 8), half)

    def spread(i):
        z_wait(i)
        x_copy(i).start()

    def project(i):
        settle()
        projected.append(i)
        if i // per_block == z:
            z_wait(i)
        x_wait(i)
        wide = jnp.concatenate([first[i, q] for q in range(n_chan)], axis=1).astype(jnp.float32)
        inv_rms = lax.rsqrt(jnp.mean(wide * wide, axis=-1, keepdims=True) + 1e-06)
        normed = (wide * inv_rms * gain_ref[...]).astype(jnp.bfloat16)
        weights = jnp.concatenate([w_in_ref[j, k] for j in range(2) for k in range(3)], axis=1)
        got = jnp.dot(normed, weights, preferred_element_type=jnp.float32).astype(jnp.bfloat16)
        stage[i] = got[:, 3 * width :]
        p_copy(i).start()
        proj[proj_rows(i, core), :] = got[:, : 3 * width].astype(jnp.float32)

    joined, formed, projected = set(), set(), []

    def join(i):
        if i in joined:
            return
        joined.add(i)
        p_copy(i).wait_recv()
        proj[proj_rows(i, 1 - core), :] = peer[i].astype(jnp.float32)

    def settle():
        for i in projected[:-1]:
            join(i)
        for i in sorted(joined):
            if i == 0 or i - 1 in joined:
                form(i)

    def form(i):
        if i in formed:
            return
        formed.add(i)
        if i > 0:
            join(i - 1)
        join(i)
        short = [jnp.concatenate([short_ref[j, k : k + 1] for k in range(3)], axis=1) for j in range(3)]
        now = proj[8 + i * width : 8 + (i + 1) * width, :]
        back1 = proj[7 + i * width : 7 + (i + 1) * width, :]
        back2 = proj[6 + i * width : 6 + (i + 1) * width, :]
        streams = short[0] * now + short[1] * back1 + short[2] * back2
        query[i] = streams[:, 0:width]
        source[i * width : (i + 1) * width, :] = (
            streams[:, width : 2 * width] * streams[:, 2 * width :]
        ).astype(jnp.bfloat16)

    def convolve(i):
        for j in range(i + 1):
            form(j)
        lane_group = lax.broadcasted_iota(jnp.int32, (width, width), 1) // group
        depth = (i + 1) * width
        sums = jnp.dot(strips[:, length - depth :], source[0:depth, :], preferred_element_type=jnp.float32)
        total = sums[0:width]
        for f in range(1, filters):
            total = jnp.where(lane_group == f, sums[f * width : (f + 1) * width], total)
        total = total + skip_ref[...] * source[i * width : (i + 1) * width, :].astype(jnp.float32)
        result = (query[i] * total).astype(jnp.bfloat16)
        for k in range(2):
            gated[i, k] = result[k * half : (k + 1) * half]
        for k in range(2):
            g_copy(i, k).start()
        g_mate(i).start()
        second[i, c] = gated[i, core]

    def mix(i):
        b = i // per_block
        g_wait(i)
        wide = jnp.concatenate([second[i, q] for q in range(n_chan)], axis=1)
        weights = jnp.concatenate([w_out[0], w_out[1]], axis=1)
        got = jnp.dot(wide, weights, preferred_element_type=jnp.float32).astype(jnp.bfloat16)
        for j in range(2):
            mixed[i, j] = got[:, j * width : (j + 1) * width]

        @when(b == z)
        def _():
            o_local(i, b).start()
            o_mate(i, b).start()

        @when(b != z)
        def _():
            for j in range(2):
                o_copy(i, j, b).start()

    proj[0:8, :] = jnp.zeros((8, proj.shape[1]), jnp.float32)
    seen = [0, 0, 0, 0]
    relayed = False
    for kind, i in STEPS[z]:
        if kind == 1 and seen[1] == 0:
            arrived(w_in_ref, got.at[4])
            for copy in fetched:
                copy.wait()
        if kind == 2 and seen[2] == 0:
            build_strips()
        if not relayed and (kind == 2 and seen[2] == 1 or kind == 3):
            relayed = True
            arrived(w_out.at[:, pl.ds(0, width)], got.at[2])
            for j in range(2):
                w_relay(j).start()
        if kind == 3 and seen[3] == 0:
            arrived(first.at[pl.ds(0, 3)], got.at[3])
        (spread, project, convolve, mix)[kind](i)
        seen[kind] += 1

    done(taps.at[pl.ds(0, n_seq - 1)], sent.at[0])
    done(recs_ref.at[pl.ds(0, n_seq - 1)], sent.at[1])
    done(recs_ref.at[0, pl.ds(0, block_len // 2)], sent.at[2])
    done(recs_ref, sent.at[3])
    done(stage, sent.at[4])
    done(second.at[pl.ds(0, 3 * per_block)], sent.at[5])
    done(recs_ref.at[pl.ds(0, n_seq - 1)], sent.at[6])
    done(recs_ref.at[0, pl.ds(0, block_len // 2)], sent.at[7])
    done(first.at[pl.ds(0, 3)], sent.at[8])
    done(w_in_hbm, sent.at[9])
    arrived(out_ref, got.at[1])


def by_record(n_seq, n_chan, records, norm_gain, in_projection, short_kernel, long_filter, skip_gain, out_projection):
    _, block_len, width = records.shape
    length = n_seq * block_len
    filters = long_filter.shape[0]
    chunks, half, per_block = length // width, width // 2, block_len // width
    hbm = pl.BlockSpec(memory_space=pltpu.HBM)
    dma = pltpu.SemaphoreType.DMA
    halves = pltpu.VMEM((chunks, n_chan, half, width), jnp.bfloat16)
    return pl.pallas_call(
        functools.partial(layer_kernel, n_seq, n_chan),
        out_shape=jax.ShapeDtypeStruct(records.shape, jnp.bfloat16),
        in_specs=[hbm] * 7,
        out_specs=hbm,
        scratch_shapes=[
            pltpu.VMEM((1, n_chan * width), jnp.float32),
            pltpu.VMEM((2, 3, n_chan * width, width), jnp.bfloat16),
            pltpu.VMEM((3, 3, width), jnp.float32),
            pltpu.VMEM((1, width), jnp.float32),
            halves,
            pltpu.VMEM((chunks, half, 3 * width), jnp.bfloat16),
            pltpu.VMEM((chunks, half, 3 * width), jnp.bfloat16),
            pltpu.VMEM((8 + length, 3 * width), jnp.float32),
            pltpu.VMEM((n_seq, filters, block_len), jnp.bfloat16),
            pltpu.VMEM((filters * width, length), jnp.bfloat16),
            pltpu.VMEM((chunks, width, width), jnp.float32),
            pltpu.VMEM((length, width), jnp.bfloat16),
            pltpu.VMEM((chunks, 2, half, width), jnp.bfloat16),
            halves,
            pltpu.VMEM((2, n_chan * width, width), jnp.bfloat16),
            pltpu.VMEM((chunks, 2, half, width), jnp.bfloat16),
            dma((chunks,)),
            dma((chunks,)),
            dma((chunks,)),
            dma((chunks,)),
            dma((8,)),
            dma((10,)),
            dma((5,)),
        ],
        compiler_params=pltpu.CompilerParams(
            collective_id=0, has_side_effects=True, vmem_limit_bytes=40 * 1024 * 1024
        ),
    )(
        *(
            pltpu.with_memory_space_constraint(value, pltpu.HBM)
            for value in (
                records,
                norm_gain[None, :],
                in_projection.transpose(1, 0, 2),
                short_kernel,
                long_filter,
                skip_gain[None, :],
                out_projection,
            )
        )
    )


def solution(mesh):
    placed = (
        P("parts", "seq", "chan"),
        P(),
        P(None, None, "chan"),
        P(None, None, "chan"),
        P("chan", "seq"),
        P("chan"),
        P("chan", None),
    )
    n_seq, n_chan, n_parts = mesh.shape["seq"], mesh.shape["chan"], mesh.shape["parts"]

    def apply(*args):
        records = args[0]
        block_len, width = records.shape[1] // n_seq, records.shape[2] // n_chan
        whole_records = records.shape[0] // n_parts == n_seq
        if whole_records and n_seq == 4 and n_chan == 4 and width == 128 and block_len % width == 0:
            chosen = functools.partial(by_record, n_seq, n_chan)
        else:
            chosen = body
        return jax.shard_map(
            chosen, mesh=mesh, in_specs=placed, out_specs=P("parts", "seq", "chan"), check_vma=False
        )(*args)

    return apply
```

```python
import functools

import jax
import jax.numpy as jnp
from jax import lax
from jax.experimental import pallas as pl
from jax.experimental.pallas import tpu as pltpu
from jax.sharding import PartitionSpec as P


def from_behind(block, axis, distance):
    devices = range(lax.axis_size(axis))
    route = [(i - distance, i) for i in devices if i - distance in devices]
    return lax.ppermute(block, axis, route)


def block_terms(taps_padded, offset, block_source, block_len):
    filter_count = taps_padded.shape[0]
    window = lax.dynamic_slice_in_dim(taps_padded, offset + 1, 2 * block_len - 1, 1)
    flipped = window[:, ::-1]
    padded = jnp.pad(flipped, ((0, 0), (0, 1)))
    tiled_taps = jnp.tile(padded, (1, block_len))
    toeplitz = tiled_taps[:, block_len - 1 : block_len - 1 + block_len * (2 * block_len - 1)]
    toeplitz = toeplitz.reshape(filter_count, block_len, 2 * block_len - 1)[:, :, :block_len]
    record_count = block_source.shape[0]
    grouped = block_source.reshape(record_count, block_len, filter_count, -1)
    return jnp.einsum("fab,rbfg->rafg", toeplitz, grouped, preferred_element_type=jnp.float32)


def body(records, norm_gain, in_projection, short_kernel, long_filter, skip_gain, out_projection):
    gathered = lax.all_gather(records, "chan", axis=2, tiled=True)
    widened = gathered.astype(jnp.float32)
    inv_rms = lax.rsqrt(jnp.mean(widened * widened, axis=-1, keepdims=True) + 1e-06)
    normed = (widened * inv_rms * norm_gain).astype(jnp.bfloat16)
    projected = jnp.einsum(
        "rtd,dkc->rtkc", normed, in_projection, preferred_element_type=jnp.float32
    ).astype(jnp.bfloat16)
    rim_rows = from_behind(projected[:, -2:], "seq", 1)
    extended = jnp.concatenate([rim_rows, projected], axis=1).astype(jnp.float32)
    streams = (
        short_kernel[0] * extended[:, 2:]
        + short_kernel[1] * extended[:, 1:-1]
        + short_kernel[2] * extended[:, :-2]
    )
    query_gate = streams[:, :, 0]
    gated_source = (streams[:, :, 1] * streams[:, :, 2]).astype(jnp.bfloat16)
    record_count = gated_source.shape[0]
    block_len = gated_source.shape[1]
    channels = gated_source.shape[2]
    all_taps = lax.all_gather(long_filter, "seq", axis=1, tiled=True)
    taps_padded = jnp.concatenate(
        [jnp.zeros((all_taps.shape[0], block_len), jnp.bfloat16), all_taps], axis=1
    )
    my_start = lax.axis_index("seq") * block_len
    cycle_stops = lax.axis_size("seq")
    long_sum = block_terms(taps_padded, 0, gated_source, block_len)

    def advance(stop_index, state):
        running_sum, visiting = state
        visiting = from_behind(visiting, "seq", 1)
        lag_start = stop_index * block_len
        running_sum = lax.cond(
            lag_start <= my_start,
            lambda running: running + block_terms(taps_padded, lag_start, visiting, block_len),
            lambda running: running,
            running_sum,
        )
        return (running_sum, visiting)

    long_sum, visiting = lax.fori_loop(1, cycle_stops, advance, (long_sum, gated_source))
    long_out = long_sum.reshape(
        record_count, block_len, channels
    ) + skip_gain * gated_source.astype(jnp.float32)
    gated = (query_gate * long_out).astype(jnp.bfloat16)
    partial_terms = jnp.einsum(
        "rtc,cd->rtd", gated, out_projection, preferred_element_type=jnp.float32
    )
    return lax.psum_scatter(
        partial_terms.astype(jnp.bfloat16), "chan", scatter_dimension=2, tiled=True
    )


MESH = pl.DeviceIdType.MESH
GIVES = (
    ((1, 0), (2, 0), (3, 0), (1, 1), (2, 1), (3, 1), (1, 2), (2, 2), (3, 2)),
    ((0, 0), (2, 0), (3, 0), (0, 1), (2, 1), (3, 1), (0, 2), (2, 2), (3, 2)),
    ((0, 0), (1, 0), (3, 0), (0, 1), (1, 1), (3, 1), (0, 2), (1, 2), (3, 2)),
    ((2, 0), (2, 1), (2, 2), (1, 0), (0, 0), (1, 1), (0, 1), (1, 2), (0, 2)),
)
STEPS = (
    ((0, 3), (1, 0), (0, 6), (1, 1), (2, 0), (0, 4), (1, 2), (2, 1), (0, 7), (2, 2), (0, 5), (0, 8), (1, 3),
     (0, 9), (1, 6), (2, 3), (3, 0), (1, 4), (0, 10), (3, 1), (2, 4), (1, 7), (0, 11), (3, 2), (1, 5), (1, 8),
     (2, 6), (2, 7), (2, 8), (3, 3), (2, 5), (1, 9), (1, 10), (3, 4), (2, 9), (2, 10), (1, 11), (3, 6), (2, 11),
     (3, 7), (3, 8), (3, 5), (3, 9), (3, 10), (3, 11)),
    ((1, 3), (1, 4), (0, 0), (0, 6), (1, 5), (0, 7), (0, 9), (0, 1), (1, 0), (1, 6), (2, 0), (1, 7), (0, 2),
     (0, 8), (1, 9), (0, 10), (1, 1), (3, 0), (0, 11), (2, 1), (1, 2), (1, 8), (2, 2), (2, 6), (2, 7), (2, 9),
     (2, 8), (3, 1), (2, 3), (2, 4), (2, 5), (3, 2), (1, 10), (3, 6), (1, 11), (3, 7), (2, 10), (2, 11), (3, 9),
     (3, 8), (3, 3), (3, 4), (3, 5), (3, 10), (3, 11)),
    ((1, 6), (0, 9), (0, 3), (1, 7), (0, 10), (1, 8), (0, 11), (0, 4), (0, 0), (1, 9), (1, 3), (0, 5), (1, 10),
     (0, 1), (1, 11), (1, 4), (1, 0), (0, 2), (1, 5), (2, 0), (1, 1), (1, 2), (2, 1), (3, 0), (2, 2), (2, 3),
     (2, 4), (2, 5), (3, 1), (2, 9), (2, 10), (3, 2), (2, 11), (3, 3), (2, 6), (2, 7), (3, 4), (2, 8), (3, 5),
     (3, 9), (3, 10), (3, 11), (3, 6), (3, 7), (3, 8)),
    ((1, 9), (0, 6), (1, 10), (0, 7), (1, 11), (0, 8), (0, 3), (1, 6), (0, 4), (1, 7), (0, 0), (1, 8), (1, 3),
     (1, 4), (0, 5), (1, 0), (0, 1), (2, 0), (1, 5), (0, 2), (1, 1), (3, 0), (2, 1), (1, 2), (2, 2), (2, 3),
     (3, 1), (2, 4), (2, 5), (2, 6), (2, 7), (3, 2), (2, 8), (2, 9), (3, 3), (2, 10), (3, 4), (2, 11), (3, 5),
     (3, 6), (3, 7), (3, 8), (3, 9), (3, 10), (3, 11)),
)


def when(condition):
    def run(act):
        if condition:
            act()

    return run


def layer_kernel(
    n_seq, n_chan, recs_ref, gain_hbm, w_in_hbm, short_hbm, taps_ref, skip_hbm, w_out_ref, out_ref,
    gain_ref, w_in_ref, short_ref, skip_ref, first, stage, peer, proj, taps, strips, query, source, gated, second,
    w_out, mixed, near, z_recv, x_recv, p_recv, g_recv, here_sem, sent, got,
):
    z = lax.axis_index("seq")
    c = lax.axis_index("chan")
    load = pltpu.make_async_copy(recs_ref, near, here_sem.at[0])
    pl.when(z < n_seq - 1)(load.start)
    barrier = pltpu.get_barrier_semaphore()
    for d in range(1, n_seq):
        for k in range(2):
            pl.semaphore_signal(
                barrier, inc=1, device_id={"seq": (z + d) % n_seq, "chan": c - c % 2 + k}, device_id_type=MESH
            )
    for d in range(1, n_chan):
        pl.semaphore_signal(barrier, inc=1, device_id={"chan": (c + d) % n_chan}, device_id_type=MESH)
    pl.semaphore_wait(barrier, 2 * (n_seq - 1) + n_chan - 1)
    for q in range(n_seq):

        @pl.when(z == q)
        def _():
            held = recs_ref
            if q < n_seq - 1:
                load.wait()
                held = near
            program(
                n_seq, n_chan, q, held, gain_hbm, w_in_hbm, short_hbm, taps_ref, skip_hbm, w_out_ref, out_ref,
                gain_ref, w_in_ref, short_ref, skip_ref, first, stage, peer, proj, taps, strips, query, source,
                gated, second, w_out, mixed, z_recv, x_recv, p_recv, g_recv, here_sem, sent, got,
            )


def program(
    n_seq, n_chan, z, recs_ref, gain_hbm, w_in_hbm, short_hbm, taps_ref, skip_hbm, w_out_ref, out_ref,
    gain_ref, w_in_ref, short_ref, skip_ref, first, stage, peer, proj, taps, strips, query, source,
    gated, second, w_out, mixed, z_recv, x_recv, p_recv, g_recv, here_sem, sent, got,
):
    block_len, width = recs_ref.shape[1], recs_ref.shape[2]
    length = n_seq * block_len
    filters = taps_ref.shape[0]
    group = width // filters
    half = width // 2
    per_block = block_len // width
    chunks = n_seq * per_block
    c = lax.axis_index("chan")
    core = c % 2
    here = c - core
    there = (here + n_chan // 2) % n_chan
    core_mate = here + 1 - core
    chip_mate = there + core

    def remote(src, dst, send, recv, **device):
        return pltpu.make_async_remote_copy(
            src_ref=src, dst_ref=dst, send_sem=send, recv_sem=recv, device_id=device, device_id_type=MESH
        )

    def rows(part, k):
        return pl.ds(pl.multiple_of(part * width + k * half, half), half)

    def f_copy(d):
        return remote(taps_ref, taps.at[z], sent.at[0], got.at[0], seq=(z + d) % n_seq)

    def z_copy(r, part, k):
        return remote(
            recs_ref.at[r, rows(part, k)], first.at[z * per_block + part, c],
            sent.at[1], z_recv.at[z * per_block + part], seq=r, chan=here + k,
        )

    def own_local(part):
        i = z * per_block + part
        return pltpu.make_async_copy(recs_ref.at[z, rows(part, core)], first.at[i, c], z_recv.at[i])

    def own_mate(part):
        i = z * per_block + part
        return remote(
            recs_ref.at[z, rows(part, 1 - core)], first.at[i, c], sent.at[2], z_recv.at[i], chan=core_mate
        )

    def own_x(part, k):
        i = z * per_block + part
        return remote(
            recs_ref.at[z, rows(part, k)], first.at[i, c], sent.at[3], x_recv.at[i], chan=there + k
        )

    def x_copy(i):
        held = first.at[i, pl.ds(here, 2)]
        return remote(held, held, sent.at[3], x_recv.at[i], chan=chip_mate)

    def z_wait(i):
        held = first.at[i, pl.ds(here, 2)]
        remote(held, held, sent.at[3], z_recv.at[i], chan=chip_mate).wait_recv()

    def x_wait(i):
        held = first.at[i, pl.ds(there, 2)]
        remote(held, held, sent.at[3], x_recv.at[i], chan=chip_mate).wait_recv()

    def p_copy(i):
        return remote(stage.at[i], peer.at[i], sent.at[4], p_recv.at[i], chan=core_mate)

    def g_copy(i, k):
        return remote(gated.at[i, k], second.at[i, c], sent.at[5], g_recv.at[i], chan=there + k)

    def g_mate(i):
        return remote(gated.at[i, 1 - core], second.at[i, c], sent.at[5], g_recv.at[i], chan=core_mate)

    def g_wait(i):
        held = second.at[i, pl.ds(0, 3)]
        remote(held, held, sent.at[5], g_recv.at[i], chan=core_mate).wait_recv()

    def o_copy(i, j, b):
        part = i - b * per_block
        return remote(
            mixed.at[i, j], out_ref.at[z, rows(part, core)], sent.at[6], got.at[1],
            seq=b, chan=core_mate if j else c,
        )

    def o_mate(i, b):
        part = i - b * per_block
        return remote(
            mixed.at[i, 1], out_ref.at[z, rows(part, core)], sent.at[7], got.at[1], chan=core_mate
        )

    def o_local(i, b):
        part = i - b * per_block
        return pltpu.make_async_copy(mixed.at[i, 0], out_ref.at[z, rows(part, core)], got.at[1])

    def columns(q):
        return pl.ds(pl.multiple_of(q * width, width), width)

    def w_x(j):
        owner = chip_mate if j == 0 else there + 1 - core
        return remote(
            w_out_ref.at[:, columns(owner)], w_out.at[j, columns(c)], sent.at[8], got.at[2], chan=chip_mate
        )

    def w_mate(j):
        owner = core_mate if j == 0 else c
        return remote(
            w_out_ref.at[:, columns(owner)], w_out.at[j, columns(c)],
            sent.at[8], got.at[3], chan=core_mate,
        )

    def w_relay(j):
        return remote(
            w_out.at[1 - j, columns(chip_mate)], w_out.at[j, columns(chip_mate)],
            sent.at[8], got.at[3], chan=core_mate,
        )

    def w_local(j):
        owner = c if j == 0 else core_mate
        return pltpu.make_async_copy(w_out_ref.at[:, columns(owner)], w_out.at[j, columns(c)], got.at[3])

    own_taps = pltpu.make_async_copy(taps_ref, taps.at[z], here_sem.at[2])
    own_w_in = pltpu.make_async_copy(w_in_hbm, w_in_ref.at[0], got.at[4])
    mate_w_in = remote(w_in_hbm, w_in_ref.at[1], sent.at[9], got.at[4], chan=core_mate)
    fetched = [
        pltpu.make_async_copy(src, dst, here_sem.at[4 + j])
        for j, (src, dst) in enumerate([(gain_hbm, gain_ref), (short_hbm, short_ref), (skip_hbm, skip_ref)])
    ]

    def done(ref, sem):
        remote(ref, ref, sem, got.at[0], chan=core_mate).wait_send()

    def arrived(ref, sem):
        remote(ref, ref, sent.at[0], sem, chan=core_mate).wait_recv()

    for d in range(1, n_seq):
        f_copy(d).start()
    for part in range(per_block):
        for k in range(2):
            own_x(part, k).start()
    for r, part in GIVES[z]:
        for k in range(2):
            z_copy(r, part, k).start()

    for part in range(per_block):
        own_local(part).start()
        own_mate(part).start()
    own_taps.start()
    own_w_in.start()
    mate_w_in.start()
    for copy in fetched:
        copy.start()
    for j in range(2):
        w_x(j).start()
        w_mate(j).start()
        w_local(j).start()

    def build_strips():
        own_taps.wait()
        arrived(taps.at[pl.ds(0, n_seq - 1)], got.at[0])
        rows = lax.broadcasted_iota(jnp.int32, (width, width), 0)
        columns = lax.broadcasted_iota(jnp.int32, (width, width), 1)
        mirror = jnp.where(rows + columns == width - 1, 1.0, 0.0).astype(jnp.bfloat16)
        pieces = []
        for s in reversed(range(n_seq)):
            held = taps[s]
            for j in reversed(range(block_len // width)):
                pieces.append(
                    jnp.dot(held[:, j * width : (j + 1) * width], mirror, preferred_element_type=jnp.float32)
                )
        pieces.append(jnp.zeros((filters, width), jnp.float32))
        backward = jnp.concatenate(pieces, axis=1)
        for f in range(filters):
            row = jnp.broadcast_to(backward[f : f + 1], (width, length + width))
            turned = pltpu.roll(row, 1, 1, stride=1, stride_axis=0)
            strips[f * width : (f + 1) * width, :] = turned[:, width:].astype(jnp.bfloat16)

    def proj_rows(i, k):
        return pl.ds(pl.multiple_of(8 + i * width + k * half, 8), half)

    def spread(i):
        z_wait(i)
        x_copy(i).start()

    def project(i):
        settle()
        projected.append(i)
        if i // per_block == z:
            z_wait(i)
        x_wait(i)
        wide = jnp.concatenate([first[i, q] for q in range(n_chan)], axis=1).astype(jnp.float32)
        inv_rms = lax.rsqrt(jnp.mean(wide * wide, axis=-1, keepdims=True) + 1e-06)
        normed = (wide * inv_rms * gain_ref[...]).astype(jnp.bfloat16)
        weights = jnp.concatenate([w_in_ref[j, k] for j in range(2) for k in range(3)], axis=1)
        got = jnp.dot(normed, weights, preferred_element_type=jnp.float32).astype(jnp.bfloat16)
        stage[i] = got[:, 3 * width :]
        p_copy(i).start()
        proj[proj_rows(i, core), :] = got[:, : 3 * width].astype(jnp.float32)

    joined, formed, projected = set(), set(), []

    def join(i):
        if i in joined:
            return
        joined.add(i)
        p_copy(i).wait_recv()
        proj[proj_rows(i, 1 - core), :] = peer[i].astype(jnp.float32)

    def settle():
        for i in projected[:-1]:
            join(i)
        for i in sorted(joined):
            if i == 0 or i - 1 in joined:
                form(i)

    def form(i):
        if i in formed:
            return
        formed.add(i)
        if i > 0:
            join(i - 1)
        join(i)
        short = [jnp.concatenate([short_ref[j, k : k + 1] for k in range(3)], axis=1) for j in range(3)]
        now = proj[8 + i * width : 8 + (i + 1) * width, :]
        back1 = proj[7 + i * width : 7 + (i + 1) * width, :]
        back2 = proj[6 + i * width : 6 + (i + 1) * width, :]
        streams = short[0] * now + short[1] * back1 + short[2] * back2
        query[i] = streams[:, 0:width]
        source[i * width : (i + 1) * width, :] = (
            streams[:, width : 2 * width] * streams[:, 2 * width :]
        ).astype(jnp.bfloat16)

    def convolve(i):
        for j in range(i + 1):
            form(j)
        lane_group = lax.broadcasted_iota(jnp.int32, (width, width), 1) // group
        depth = (i + 1) * width
        sums = jnp.dot(strips[:, length - depth :], source[0:depth, :], preferred_element_type=jnp.float32)
        total = sums[0:width]
        for f in range(1, filters):
            total = jnp.where(lane_group == f, sums[f * width : (f + 1) * width], total)
        total = total + skip_ref[...] * source[i * width : (i + 1) * width, :].astype(jnp.float32)
        result = (query[i] * total).astype(jnp.bfloat16)
        for k in range(2):
            gated[i, k] = result[k * half : (k + 1) * half]
        for k in range(2):
            g_copy(i, k).start()
        g_mate(i).start()
        second[i, c] = gated[i, core]

    def mix(i):
        b = i // per_block
        g_wait(i)
        wide = jnp.concatenate([second[i, q] for q in range(n_chan)], axis=1)
        weights = jnp.concatenate([w_out[0], w_out[1]], axis=1)
        got = jnp.dot(wide, weights, preferred_element_type=jnp.float32).astype(jnp.bfloat16)
        for j in range(2):
            mixed[i, j] = got[:, j * width : (j + 1) * width]

        @when(b == z)
        def _():
            o_local(i, b).start()
            o_mate(i, b).start()

        @when(b != z)
        def _():
            for j in range(2):
                o_copy(i, j, b).start()

    proj[0:8, :] = jnp.zeros((8, proj.shape[1]), jnp.float32)
    seen = [0, 0, 0, 0]
    relayed = False
    for kind, i in STEPS[z]:
        if kind == 1 and seen[1] == 0:
            arrived(w_in_ref, got.at[4])
            for copy in fetched:
                copy.wait()
        if kind == 2 and seen[2] == 0:
            build_strips()
        if not relayed and (kind == 2 and seen[2] == 1 or kind == 3):
            relayed = True
            arrived(w_out.at[:, pl.ds(0, width)], got.at[2])
            for j in range(2):
                w_relay(j).start()
        if kind == 3 and seen[3] == 0:
            arrived(first.at[pl.ds(0, 3)], got.at[3])
        (spread, project, convolve, mix)[kind](i)
        seen[kind] += 1

    done(taps.at[pl.ds(0, n_seq - 1)], sent.at[0])
    done(recs_ref.at[pl.ds(0, n_seq - 1)], sent.at[1])
    done(recs_ref.at[0, pl.ds(0, block_len // 2)], sent.at[2])
    done(recs_ref, sent.at[3])
    done(stage, sent.at[4])
    done(second.at[pl.ds(0, 3 * per_block)], sent.at[5])
    done(recs_ref.at[pl.ds(0, n_seq - 1)], sent.at[6])
    done(recs_ref.at[0, pl.ds(0, block_len // 2)], sent.at[7])
    done(first.at[pl.ds(0, 3)], sent.at[8])
    done(w_in_hbm, sent.at[9])
    arrived(out_ref, got.at[1])


def by_record(n_seq, n_chan, records, norm_gain, in_projection, short_kernel, long_filter, skip_gain, out_projection):
    _, block_len, width = records.shape
    length = n_seq * block_len
    filters = long_filter.shape[0]
    chunks, half, per_block = length // width, width // 2, block_len // width
    hbm = pl.BlockSpec(memory_space=pltpu.HBM)
    dma = pltpu.SemaphoreType.DMA
    halves = pltpu.VMEM((chunks, n_chan, half, width), jnp.bfloat16)
    return pl.pallas_call(
        functools.partial(layer_kernel, n_seq, n_chan),
        out_shape=jax.ShapeDtypeStruct(records.shape, jnp.bfloat16),
        in_specs=[hbm] * 7,
        out_specs=hbm,
        scratch_shapes=[
            pltpu.VMEM((1, n_chan * width), jnp.float32),
            pltpu.VMEM((2, 3, n_chan * width, width), jnp.bfloat16),
            pltpu.VMEM((3, 3, width), jnp.float32),
            pltpu.VMEM((1, width), jnp.float32),
            halves,
            pltpu.VMEM((chunks, half, 3 * width), jnp.bfloat16),
            pltpu.VMEM((chunks, half, 3 * width), jnp.bfloat16),
            pltpu.VMEM((8 + length, 3 * width), jnp.float32),
            pltpu.VMEM((n_seq, filters, block_len), jnp.bfloat16),
            pltpu.VMEM((filters * width, length), jnp.bfloat16),
            pltpu.VMEM((chunks, width, width), jnp.float32),
            pltpu.VMEM((length, width), jnp.bfloat16),
            pltpu.VMEM((chunks, 2, half, width), jnp.bfloat16),
            halves,
            pltpu.VMEM((2, n_chan * width, width), jnp.bfloat16),
            pltpu.VMEM((chunks, 2, half, width), jnp.bfloat16),
            pltpu.VMEM(records.shape, jnp.bfloat16),
            dma((chunks,)),
            dma((chunks,)),
            dma((chunks,)),
            dma((chunks,)),
            dma((8,)),
            dma((10,)),
            dma((5,)),
        ],
        compiler_params=pltpu.CompilerParams(
            collective_id=0, has_side_effects=True, vmem_limit_bytes=40 * 1024 * 1024
        ),
    )(
        *(
            pltpu.with_memory_space_constraint(value, pltpu.HBM)
            for value in (
                records,
                norm_gain[None, :],
                in_projection.transpose(1, 0, 2),
                short_kernel,
                long_filter,
                skip_gain[None, :],
                out_projection,
            )
        )
    )


def solution(mesh):
    placed = (
        P("parts", "seq", "chan"),
        P(),
        P(None, None, "chan"),
        P(None, None, "chan"),
        P("chan", "seq"),
        P("chan"),
        P("chan", None),
    )
    n_seq, n_chan, n_parts = mesh.shape["seq"], mesh.shape["chan"], mesh.shape["parts"]

    def apply(*args):
        records = args[0]
        block_len, width = records.shape[1] // n_seq, records.shape[2] // n_chan
        whole_records = records.shape[0] // n_parts == n_seq
        if whole_records and n_seq == 4 and n_chan == 4 and width == 128 and block_len % width == 0:
            chosen = functools.partial(by_record, n_seq, n_chan)
        else:
            chosen = body
        return jax.shard_map(
            chosen, mesh=mesh, in_specs=placed, out_specs=P("parts", "seq", "chan"), check_vma=False
        )(*args)

    return apply
```
